32 devices in a mesh: expert: 4 (over z), shard: 8 (over y, x, core).
Axes of the slice: x: 2, y: 2, z: 4, core: 2. Of those that a mesh axis runs over, the one named last changes fastest.
Arguments:
- tokens: bfloat16 [4096, 2048], P(('expert', 'shard')), may hold values from -6 to 6
- attn_gain: bfloat16 [2048], P('shard'), may hold values from 0.5 to 1.5
- qkv_weight: bfloat16 [2048, 3, 2048], P(None, None, 'shard'), may hold values from -0.125 to 0.125
- qkv_bias: bfloat16 [3, 2048], P(None, 'shard'), may hold values from -3 to 3
- out_weight: bfloat16 [2048, 2048], P('shard'), may hold values from -1 to 1
- ffn_gain: bfloat16 [2048], P('shard'), may hold values from 0.5 to 1.5
- router_weight: bfloat16 [2048, 8], P('shard'), may hold values from -0.125 to 0.125
- shared_gate_weight: bfloat16 [2048], P('shard'), may hold values from -0.125 to 0.125
- shared_weights: bfloat16 [3, 2048, 5632], P(None, None, 'shard'), may hold values from -0.125 to 0.125
- expert_gate_up: bfloat16 [2048, 8, 2816], P('shard', 'expert'), may hold values from -0.125 to 0.125
- expert_down: bfloat16 [1408, 8, 2048], P('shard', 'expert'), may hold values from -0.15625 to 0.15625
- routes: int32 [4096, 4], P(('expert', 'shard')), may hold values from 0 to 7, all different within a row
- arrival: int32 [32, 512], P(('expert', 'shard')), may hold values from 0 to 511, each once within a row
- cotangent: bfloat16 [4096, 2048], P(('expert', 'shard')), may hold values from -6 to 6
Outputs:
- output: bfloat16 [4096, 2048], P(('expert', 'shard'))
- tokens_grad: bfloat16 [4096, 2048], P(('expert', 'shard'))
- attn_gain_grad: float32 [2048], P('shard')
- qkv_weight_grad: float32 [2048, 3, 2048], P(None, None, 'shard')
- qkv_bias_grad: float32 [3, 2048], P(None, 'shard')
- out_weight_grad: float32 [2048, 2048], P('shard')
- ffn_gain_grad: float32 [2048], P('shard')
- router_weight_grad: float32 [2048, 8], P('shard')
- shared_gate_weight_grad: float32 [2048], P('shard')
- shared_weights_grad: float32 [3, 2048, 5632], P(None, None, 'shard')
- expert_gate_up_grad: float32 [2048, 8, 2816], P('shard', 'expert')
- expert_down_grad: float32 [1408, 8, 2048], P('shard', 'expert')
The draws below stay inside these ranges and needn't reach their ends.
Inputs may be any that keep to these rules, and one draw needn't show every extreme that they name: `routes`: each row names 4 different experts. `arrival`: each row is a permutation.
All inputs are finite; a program needn't handle non-finite values.
Results may differ from the reference program's by a relative error of at most 0.018.
The reference program's roundings to bfloat16 on the way count: a program that leaves them out, or rounds other values in their place, can miss the bound.
Values may be sent and summed in bfloat16 or wider, within the bound.
No kernel may reach another device: no remote copies, remote signals or barrier semaphores. Data moves between devices by JAX's collectives and lax.ppermute only.
A program may use at most 320 MiB of HBM per device.

```python
from functools import partial
import jax
import jax.numpy as jnp
from jax import lax

D = 2048
HEADS = 16
HEAD_DIM = 128
SHARED_FF = 5632
EXPERT_FF = 1408
TOPK = 4
TOK_DEV = 128
EXPERTS = 8
GROUP_TOKENS = 1024
PROMPT = 512
TOKENS = 4096
CAPACITY = 64
N_EXPERT = 4
N_SHARD = 8


def shard_levels(key, shape, pieces, least, largest):
    factor_of, own = 1.0, jax.random.fold_in(key, 6)
    for axis_at, parts in pieces:
        draws = jnp.exp(jax.random.uniform(jax.random.fold_in(own, axis_at), (parts,), jnp.float32, least / len(pieces), largest / len(pieces)))
        factor_of = factor_of * jnp.repeat(draws, shape[axis_at] // parts).reshape([-1 if axis == axis_at else 1 for axis in range(len(shape))])
    return factor_of


def distinct(key, rows, amount, top, lift):
    ranking = jax.random.permutation(jax.random.fold_in(key, 1), amount)
    boost = ranking
    for power in range(3):
        boost = boost * boost // amount
    boost = boost * lift // amount
    lots = jax.random.randint(jax.random.fold_in(key, 2), (rows, amount), 0, 4096) + boost
    fixed_rows = jax.random.permutation(jax.random.fold_in(key, 3), rows)[jnp.arange(amount) % rows]
    lots = jnp.where(jnp.arange(rows)[:, None] == fixed_rows[None, :], 1 << 14, lots)
    score = lots * amount + jnp.arange(amount)
    return lax.top_k(score.astype(jnp.int32), top)[1].astype(jnp.int32)


def gaussian(stream_key, shape, deviation, reach, shards=(), kind=jnp.bfloat16):
    values = deviation * jax.random.normal(stream_key, shape, jnp.float32)
    if shards:
        values = values * shard_levels(stream_key, shape, shards, -0.22, 0.18)
    return jnp.clip(values, -reach, reach).astype(kind)


def setup_inputs(seed: int = 0) -> dict:
    streams_of = jax.random.split(jax.random.key(seed), 15)
    return {
        "tokens": gaussian(streams_of[0], (TOKENS, D), 1.0, 6.0, ((0, 32),)),
        "attn_gain": jnp.clip(1.0 + 0.1 * jax.random.normal(streams_of[1], (D,), jnp.float32), 0.5, 1.5).astype(jnp.bfloat16),
        "qkv_weight": gaussian(streams_of[2], (D, 3, D), D ** -0.5, 0.125, ((2, 8),)),
        "qkv_bias": gaussian(streams_of[3], (3, D), 0.5, 3.0, ((1, 8),)),
        "out_weight": gaussian(streams_of[4], (D, D), (D // 64) ** -0.5, 1.0, ((0, 8),)),
        "ffn_gain": jnp.clip(1.0 + 0.1 * jax.random.normal(streams_of[5], (D,), jnp.float32), 0.5, 1.5).astype(jnp.bfloat16),
        "router_weight": gaussian(streams_of[6], (D, EXPERTS), D ** -0.5, 0.125, ((0, 8),)),
        "shared_gate_weight": gaussian(streams_of[7], (D,), D ** -0.5, 0.125, ((0, 8),)),
        "shared_weights": gaussian(streams_of[8], (3, D, SHARED_FF), D ** -0.5, 0.125, ((2, 8),)),
        "expert_gate_up": gaussian(streams_of[9], (D, EXPERTS, 2 * EXPERT_FF), D ** -0.5, 0.125, ((0, 8), (1, 4))),
        "expert_down": gaussian(streams_of[10], (EXPERT_FF, EXPERTS, D), EXPERT_FF ** -0.5, 0.15625, ((0, 8), (1, 4))),
        "routes": distinct(streams_of[11], TOKENS, EXPERTS, TOPK, 4096),
        "arrival": jax.vmap(lambda own: jax.random.permutation(own, TOK_DEV * TOPK))(jax.random.split(streams_of[12], (N_EXPERT * N_SHARD))).reshape((N_EXPERT * N_SHARD, TOK_DEV * TOPK)).astype(jnp.int32),
        "cotangent": gaussian(streams_of[13], (TOKENS, D), 1.0, 6.0, ((0, 32),)),
    }


@jax.custom_vjp
def low(v):
    return lax.optimization_barrier(v.astype(jnp.bfloat16)).astype(jnp.float32)

@jax.custom_vjp
def low_back(v):
    return v

def low_keep(v):
    return (low(v), None)

def low_pass(kept, grad):
    return (grad,)

def back_keep(v):
    return (v, None)

def back_low(kept, grad):
    return (low(grad),)
low.defvjp(low_keep, low_pass)
low_back.defvjp(back_keep, back_low)
EPSILON = 1e-06
ROPE_BASE = 1000000.0
MASKED = -1e+30

def matmul_high(left, right):
    return jnp.dot(left, right, precision=lax.Precision.HIGHEST, preferred_element_type=jnp.float32)

def swish(values):
    return values / (1.0 + jnp.exp(-values))

def normed(values):
    return values * lax.rsqrt(lax.optimization_barrier(jnp.mean(values * values, axis=1, keepdims=True)) + EPSILON)

def softmax_rows(scores):
    top = lax.optimization_barrier(jnp.max(scores, axis=-1, keepdims=True))
    expo = jnp.exp(scores - top)
    return expo / lax.optimization_barrier(jnp.sum(expo, axis=-1, keepdims=True))

def rope_tables(positions):
    half = HEAD_DIM // 2
    freq = ROPE_BASE ** (-jnp.arange(half, dtype=jnp.float32) * 2.0 / HEAD_DIM)
    angle_tab = positions.astype(jnp.float32)[:, None] * freq[None, :]
    cosine = jnp.cos(angle_tab)
    sine = jnp.sin(angle_tab)
    return (jnp.concatenate([cosine, cosine], 1), jnp.concatenate([sine, sine], 1))

def rotate(values, cosine, sine):
    half = HEAD_DIM // 2
    turned = jnp.concatenate([-values[..., half:], values[..., :half]], -1)
    return values * cosine[:, None, :] + turned * sine[:, None, :]

def visible(query_rows, key_rows):
    query_col = query_rows[:, None]
    key_line = key_rows[None, :]
    prompt_key = key_line < PROMPT
    same_cont = (key_line >= PROMPT) & (query_col >= PROMPT) & ((key_line - PROMPT) // TOK_DEV == (query_col - PROMPT) // TOK_DEV)
    return prompt_key & ((query_col >= PROMPT) | (key_line <= query_col)) | same_cont & (key_line <= query_col)

def attend_group(operands):
    group_q, group_k, group_v = operands
    rows = jnp.arange(GROUP_TOKENS, dtype=jnp.int32)
    allowed = visible(rows, rows)

    def one_head(head_ops):
        q_head, k_head, v_head = head_ops
        scores = low_back(matmul_high(q_head, k_head.T) * HEAD_DIM ** (-0.5))
        scores = jnp.where(allowed, scores, MASKED)
        probs = softmax_rows(scores)
        return matmul_high(low(probs), v_head)
    mapped = lax.map(jax.checkpoint(one_head), (jnp.transpose(group_q, (1, 0, 2)), jnp.transpose(group_k, (1, 0, 2)), jnp.transpose(group_v, (1, 0, 2))))
    return jnp.transpose(mapped, (1, 0, 2))

def slot_table(routes, arrival):
    per_device = routes.reshape(N_EXPERT * N_SHARD, TOK_DEV * TOPK)

    def ranks_of(operands):
        ids, prio = operands
        same = ids[:, None] == ids[None, :]
        earlier = prio[None, :] < prio[:, None]
        return lax.optimization_barrier(jnp.sum((same & earlier).astype(jnp.int32), axis=1))
    ranks = lax.map(ranks_of, (per_device, arrival))
    device_ids = jnp.arange(N_EXPERT * N_SHARD, dtype=jnp.int32)[:, None]
    assign = jnp.arange(TOKENS * TOPK, dtype=jnp.int32).reshape(N_EXPERT * N_SHARD, TOK_DEV * TOPK)
    slots = jnp.where(ranks < CAPACITY, device_ids * CAPACITY + ranks, N_EXPERT * N_SHARD * CAPACITY)
    table = jnp.full((EXPERTS, N_EXPERT * N_SHARD * CAPACITY), TOKENS * TOPK, jnp.int32)
    return table.at[per_device.reshape(-1), slots.reshape(-1)].set(assign.reshape(-1), mode='drop')

def forward(table, tokens, attn_gain, qkv_weight, qkv_bias, out_weight, ffn_gain, router_weight, shared_gate_weight, shared_weights, expert_gate_up, expert_down):
    attn_in = low(normed(tokens) * attn_gain)
    qkv = low_back(matmul_high(attn_in, qkv_weight.reshape(D, 3 * D)) + qkv_bias.reshape(3 * D))
    rows = jnp.arange(TOKENS, dtype=jnp.int32) % GROUP_TOKENS
    positions = jnp.where(rows < PROMPT, rows, PROMPT + (rows - PROMPT) % TOK_DEV)
    cosine, sine = rope_tables(positions)
    split_shape = (TOKENS, HEADS, HEAD_DIM)
    queries = low(rotate(qkv[:, :D].reshape(split_shape), cosine, sine))
    keys_all = low(rotate(qkv[:, D:2 * D].reshape(split_shape), cosine, sine))
    values_all = low(qkv[:, 2 * D:].reshape(split_shape))
    groups = TOKENS // GROUP_TOKENS
    group_shape = (groups, GROUP_TOKENS, HEADS, HEAD_DIM)
    context = lax.map(jax.checkpoint(attend_group), (queries.reshape(group_shape), keys_all.reshape(group_shape), values_all.reshape(group_shape)))
    context = low(low_back(context.reshape(TOKENS, D)))
    hidden_state = tokens + low_back(matmul_high(context, out_weight))
    ffn_in = low(normed(hidden_state) * ffn_gain)
    router = softmax_rows(low_back(matmul_high(ffn_in, router_weight)))
    gate_up = low_back(matmul_high(ffn_in, jnp.concatenate([shared_weights[0], shared_weights[1]], 1)))
    shared_hidden = low(swish(gate_up[:, :SHARED_FF]) * gate_up[:, SHARED_FF:])
    shared_out = low_back(matmul_high(shared_hidden, shared_weights[2].T))
    gate_logit = matmul_high(ffn_in, shared_gate_weight[:, None])
    shared_scale = 1.0 / (1.0 + jnp.exp(-gate_logit))
    ffn_pad = jnp.concatenate([ffn_in, jnp.zeros((1, D), jnp.float32)], 0)
    router_pad = jnp.concatenate([router, jnp.zeros((1, EXPERTS), jnp.float32)], 0)
    token_of = table // TOPK

    def expert_rows(operands):
        ids, gate_up_e, down_e = operands
        rows_in = low_back(ffn_pad[ids])
        both = low_back(matmul_high(rows_in, gate_up_e))
        hidden_e = low(swish(both[:, :EXPERT_FF]) * both[:, EXPERT_FF:])
        return low(low_back(matmul_high(hidden_e, down_e)))
    expert_out = lax.map(jax.checkpoint(expert_rows), (token_of, jnp.transpose(expert_gate_up, (1, 0, 2)), jnp.transpose(expert_down, (1, 0, 2))))
    weight = router_pad[token_of, jnp.arange(EXPERTS, dtype=jnp.int32)[:, None]]
    contrib = weight[:, :, None] * expert_out
    routed = jnp.zeros((TOKENS + 1, D), jnp.float32).at[token_of.reshape(-1)].add(contrib.reshape(-1, D))[:TOKENS]
    return hidden_state + routed + shared_scale * shared_out

def reference(tokens, attn_gain, qkv_weight, qkv_bias, out_weight, ffn_gain, router_weight, shared_gate_weight, shared_weights, expert_gate_up, expert_down, routes, arrival, cotangent):
    table = slot_table(routes, arrival)
    floats = (tokens.astype(jnp.float32), attn_gain.astype(jnp.float32), qkv_weight.astype(jnp.float32), qkv_bias.astype(jnp.float32), out_weight.astype(jnp.float32), ffn_gain.astype(jnp.float32), router_weight.astype(jnp.float32), shared_gate_weight.astype(jnp.float32), shared_weights.astype(jnp.float32), expert_gate_up.astype(jnp.float32), expert_down.astype(jnp.float32))
    output, pullback = jax.vjp(partial(forward, table), *floats)
    grads = pullback(cotangent.astype(jnp.float32))
    return (output.astype(jnp.bfloat16), grads[0].astype(jnp.bfloat16), grads[1], grads[2], grads[3], grads[4], grads[5], grads[6], grads[7], grads[8], grads[9], grads[10])
```

```python
import functools
import jax
import jax.numpy as jnp
from jax import lax
from jax.experimental import pallas as pl
from jax.experimental.pallas import tpu as pltpu
from jax.sharding import PartitionSpec as P

HEADS = 16
HEAD_DIM = 128
EXPERT_FF = 1408
TOPK = 4
LANES = 128
EPSILON = 1e-06
ROPE_BASE = 1000000.0
MASKED = -1e30
F32 = jnp.float32
BF16 = jnp.bfloat16
NN = ((1,), (0,))
NT = ((1,), (1,))
TN = ((0,), (0,))
VMEM_LIMIT = 60 << 20


def dot(left, right, dims):
    return lax.dot_general(left, right, (dims, ((), ())), preferred_element_type=F32)


def logistic(values):
    return 1.0 / (1.0 + jnp.exp(-values))


def params(*order):
    return pltpu.CompilerParams(dimension_semantics=order, vmem_limit_bytes=VMEM_LIMIT)


def cost(flops, nbytes, special=0):
    return pl.CostEstimate(flops=int(flops), bytes_accessed=int(nbytes), transcendentals=int(special))


def qkv_body(block, blocks_ref, x_ref, gain_ref, w_ref, bias_ref, cos_ref, sin_ref, qkv_ref, attn_t_ref):
    step = pl.program_id(0)
    x = x_ref[...].astype(F32)
    inv = lax.rsqrt(jnp.mean(x * x, axis=1, keepdims=True) + EPSILON)
    attn_in = (x * inv * gain_ref[...]).astype(BF16)
    attn_t_ref[...] = attn_in.T
    cols = w_ref.shape[2]
    per_step = x.shape[0] // block
    for part in range(3):
        heads = dot(attn_in, w_ref[part], NN) + bias_ref[part : part + 1].astype(F32)
        for b in range(per_step):
            row = pl.multiple_of(blocks_ref[step * per_step + b] * block, block)
            own = heads[b * block : (b + 1) * block]
            if part < 2:
                cosine = cos_ref[pl.ds(row, block)]
                sine = sin_ref[pl.ds(row, block)]
                turned = []
                for h in range(cols // HEAD_DIM):
                    one = own[:, h * HEAD_DIM : (h + 1) * HEAD_DIM]
                    turned.append(one * cosine + pltpu.roll(one, HEAD_DIM // 2, 1) * sine)
                own = jnp.concatenate(turned, 1) if len(turned) > 1 else turned[0]
            qkv_ref[pl.ds(row, block), part * cols : (part + 1) * cols] = own.astype(BF16)


def qkv_forward(x_all, gain, w_three, bias, cosine, sine_signed, blocks, block):
    rows, width = x_all.shape
    cols = w_three.shape[2]
    tile = 2 * block
    whole = lambda *shape: pl.BlockSpec(shape, lambda i, b: (0,) * len(shape))
    return pl.pallas_call(
        functools.partial(qkv_body, block),
        grid_spec=pltpu.PrefetchScalarGridSpec(
            num_scalar_prefetch=1,
            grid=(rows // tile,),
            in_specs=[
                pl.BlockSpec((tile, width), lambda i, b: (i, 0)),
                whole(1, width),
                whole(3, width, cols),
                whole(3, cols),
                whole(rows, HEAD_DIM),
                whole(rows, HEAD_DIM),
            ],
            out_specs=[
                whole(rows, 3 * cols),
                pl.BlockSpec((width, tile), lambda i, b: (0, i)),
            ],
        ),
        out_shape=[
            jax.ShapeDtypeStruct((rows, 3 * cols), BF16),
            jax.ShapeDtypeStruct((width, rows), BF16),
        ],
        compiler_params=params("arbitrary"),
        cost_estimate=cost(6 * rows * width * cols, 4 * rows * width + 6 * width * cols),
        name="qkv_forward",
    )(blocks, x_all, gain, w_three, bias, cosine, sine_signed)


def tile_mask(tile, cont, inside):
    query = lax.broadcasted_iota(jnp.int32, (tile, tile), 0)
    key = lax.broadcasted_iota(jnp.int32, (tile, tile), 1)
    ok = key <= query
    if inside:
        ok = ok & (query // cont == key // cont)
    return ok


def attend_body(block, prompt, blocks_ref, q_ref, k_ref, v_ref, ctx_ref, ctx_t_ref):
    rows = q_ref.shape[0]
    tile = 2 * block
    scale = HEAD_DIM ** (-0.5)
    for t in range(rows // tile):
        at = t * tile
        own = slice(at, at + tile)
        before = min(at, prompt)
        q = q_ref[own]
        near = dot(q, k_ref[own], NT) * scale
        near = jnp.where(tile_mask(tile, block, at >= prompt), near, MASKED)
        if before:
            scores = jnp.concatenate([dot(q, k_ref[:before], NT) * scale, near], 1)
        else:
            scores = near
        top = jnp.max(scores, axis=1, keepdims=True)
        expo = jnp.exp(scores - top)
        probs = (expo / jnp.sum(expo, axis=1, keepdims=True)).astype(BF16)
        mixed = dot(probs[:, before:], v_ref[own], NN)
        if before:
            mixed = mixed + dot(probs[:, :before], v_ref[:before], NN)
        mixed = mixed.astype(BF16)
        mixed_t = mixed.T
        for b in range(2):
            row = pl.multiple_of(blocks_ref[2 * t + b] * block, block)
            ctx_ref[pl.ds(row, block)] = mixed[b * block : (b + 1) * block]
            ctx_t_ref[:, pl.ds(row, block)] = mixed_t[:, b * block : (b + 1) * block]


def attend_forward(qkv, blocks, block, prompt):
    rows = qkv.shape[0]
    heads = qkv.shape[1] // (3 * HEAD_DIM)
    spec = lambda off: pl.BlockSpec((rows, HEAD_DIM), lambda h, b: (0, off + h))
    return pl.pallas_call(
        functools.partial(attend_body, block, prompt),
        grid_spec=pltpu.PrefetchScalarGridSpec(
            num_scalar_prefetch=1,
            grid=(heads,),
            in_specs=[spec(0), spec(heads), spec(2 * heads)],
            out_specs=[spec(0), pl.BlockSpec((HEAD_DIM, rows), lambda h, b: (h, 0))],
        ),
        out_shape=[
            jax.ShapeDtypeStruct((rows, heads * HEAD_DIM), BF16),
            jax.ShapeDtypeStruct((heads * HEAD_DIM, rows), BF16),
        ],
        compiler_params=params("arbitrary"),
        cost_estimate=cost(2.4 * rows * rows * heads * HEAD_DIM, 8 * rows * heads * HEAD_DIM, rows * rows * heads * 0.6),
        name="attend_forward",
    )(blocks, qkv, qkv, qkv)


def attend_back_body(block, prompt, blocks_ref, q_ref, k_ref, v_ref, g_ref, cos_ref, sin_ref, out_ref, dk_ref, dv_ref):
    rows = q_ref.shape[0]
    tile = 2 * block
    half = HEAD_DIM // 2
    scale = HEAD_DIM ** (-0.5)
    dk_ref[...] = jnp.zeros_like(dk_ref)
    dv_ref[...] = jnp.zeros_like(dv_ref)

    def store(part, at, value):
        for b in range(2):
            row = pl.multiple_of(blocks_ref[at // block + b] * block, block)
            out_ref[part, pl.ds(row, block)] = value[b * block : (b + 1) * block].astype(BF16)

    def unturn(value, at):
        cosine = cos_ref[at : at + tile]
        scaled = value * sin_ref[at : at + tile]
        return value * cosine + pltpu.roll(scaled, half, 1)

    for t in range(rows // tile):
        at = t * tile
        own = slice(at, at + tile)
        before = min(at, prompt)
        q = q_ref[own]
        grads = []
        for b in range(2):
            row = pl.multiple_of(blocks_ref[2 * t + b] * block, block)
            grads.append(g_ref[pl.ds(row, block)])
        g = jnp.concatenate(grads, 0)
        key = lax.broadcasted_iota(jnp.int32, (tile, tile), 0)
        query = lax.broadcasted_iota(jnp.int32, (tile, tile), 1)
        ok = key <= query
        if at >= prompt:
            ok = ok & (query // block == key // block)
        near = jnp.where(ok, dot(k_ref[own], q, NT) * scale, MASKED)
        d_near = dot(v_ref[own], g, NT)
        if before:
            scores = jnp.concatenate([dot(k_ref[:before], q, NT) * scale, near], 0)
            d_probs = jnp.concatenate([dot(v_ref[:before], g, NT), d_near], 0)
        else:
            scores, d_probs = near, d_near
        top = jnp.max(scores, axis=0, keepdims=True)
        expo = jnp.exp(scores - top)
        probs = expo / jnp.sum(expo, axis=0, keepdims=True)
        delta = jnp.sum(d_probs * probs, axis=0, keepdims=True)
        d_scores = (probs * (d_probs - delta)).astype(BF16)
        probs = probs.astype(BF16)
        dq = dot(d_scores[before:], k_ref[own], TN)
        if before:
            dq = dq + dot(d_scores[:before], k_ref[:before], TN)
            dk_ref[:before] += dot(d_scores[:before], q, NN)
            dv_ref[:before] += dot(probs[:before], g, NN)
        dk_ref[own] += dot(d_scores[before:], q, NN)
        dv_ref[own] += dot(probs[before:], g, NN)
        store(0, at, unturn(dq * scale, at))
    for t in range(rows // tile):
        at = t * tile
        own = slice(at, at + tile)
        store(1, at, unturn(dk_ref[own] * scale, at))
        store(2, at, dv_ref[own])


def attend_backward(qkv, d_ctx, cosine, sine_back, blocks, block, prompt):
    rows = qkv.shape[0]
    heads = qkv.shape[1] // (3 * HEAD_DIM)
    spec = lambda off: pl.BlockSpec((rows, HEAD_DIM), lambda h, b: (0, off + h))
    table = pl.BlockSpec((rows, HEAD_DIM), lambda h, b: (0, 0))
    return pl.pallas_call(
        functools.partial(attend_back_body, block, prompt),
        grid_spec=pltpu.PrefetchScalarGridSpec(
            num_scalar_prefetch=1,
            grid=(heads,),
            in_specs=[spec(0), spec(heads), spec(2 * heads), spec(0), table, table],
            out_specs=pl.BlockSpec((3, rows, HEAD_DIM), lambda h, b: (0, 0, h)),
            scratch_shapes=[pltpu.VMEM((rows, HEAD_DIM), F32)] * 2,
        ),
        out_shape=jax.ShapeDtypeStruct((3, rows, heads * HEAD_DIM), BF16),
        compiler_params=params("arbitrary"),
        cost_estimate=cost(6 * rows * rows * heads * HEAD_DIM, 16 * rows * heads * HEAD_DIM, rows * rows * heads * 0.6),
        name="attend_backward",
    )(blocks, qkv, qkv, qkv, d_ctx, cosine, sine_back)


def input_grad_body(d_ref, w_ref, out_ref):
    total = dot(d_ref[0], w_ref[0], NT)
    for part in range(1, 3):
        total = total + dot(d_ref[part], w_ref[part], NT)
    out_ref[...] = total.astype(BF16)


def input_grad(d_qkv, w_three):
    _, rows, cols = d_qkv.shape
    width = w_three.shape[1]
    tile = 256
    return pl.pallas_call(
        input_grad_body,
        grid=(rows // tile,),
        in_specs=[
            pl.BlockSpec((3, tile, cols), lambda i: (0, i, 0)),
            pl.BlockSpec((3, width, cols), lambda i: (0, 0, 0)),
        ],
        out_specs=pl.BlockSpec((tile, width), lambda i: (i, 0)),
        out_shape=jax.ShapeDtypeStruct((rows, width), BF16),
        compiler_params=params("arbitrary"),
        cost_estimate=cost(6 * rows * width * cols, 2 * rows * width + 6 * width * cols),
        name="input_grad",
    )(d_qkv, w_three)


def shared_body(x_ref, dy_ref, wz_ref, w_ref, back_ref, out_ref, d_so_ref, sh_t_ref, dg_t_ref, du_t_ref):
    x = x_ref[...]
    dy = dy_ref[...].astype(F32)
    z = logistic(jnp.sum(x.astype(F32) * wz_ref[...], axis=1, keepdims=True))
    d_so = (z * dy).astype(BF16)
    d_so_ref[...] = d_so
    gate = dot(x, w_ref[0], NT)
    up = dot(x, w_ref[1], NT)
    sig = logistic(gate)
    act = gate * sig
    hidden = (act * up).astype(BF16)
    sh_t_ref[...] = hidden.T
    d_sh = dot(d_so, w_ref[2], NT)
    d_gate = (d_sh * up * (sig * (1.0 + gate * (1.0 - sig)))).astype(BF16)
    d_up = (d_sh * act).astype(BF16)
    dg_t_ref[...] = d_gate.T
    du_t_ref[...] = d_up.T
    width = x.shape[1]
    back_ref[:, :width] = (dot(d_gate, w_ref[0], NN) + dot(d_up, w_ref[1], NN)).astype(BF16)
    out = dot(hidden, w_ref[2], NN)
    out_ref[...] = out.astype(BF16)
    dz = jnp.sum(dy * out, axis=1, keepdims=True)
    lane = lax.broadcasted_iota(jnp.int32, (x.shape[0], LANES), 1)
    back_ref[:, width:] = jnp.where(lane == 0, dz, 0.0).astype(BF16)


def shared_expert(x_all, dy_all, wz, w_three):
    rows, width = x_all.shape
    ff = w_three.shape[1]
    tile = 256
    row_spec = pl.BlockSpec((tile, width), lambda i: (i, 0))
    col_spec = pl.BlockSpec((ff, tile), lambda i: (0, i))
    return pl.pallas_call(
        shared_body,
        grid=(rows // tile,),
        in_specs=[
            row_spec,
            row_spec,
            pl.BlockSpec((1, width), lambda i: (0, 0)),
            pl.BlockSpec((3, ff, width), lambda i: (0, 0, 0)),
        ],
        out_specs=[
            pl.BlockSpec((tile, width + LANES), lambda i: (i, 0)),
            row_spec,
            row_spec,
            col_spec,
            col_spec,
            col_spec,
        ],
        out_shape=[jax.ShapeDtypeStruct((rows, width + LANES), BF16)]
        + [jax.ShapeDtypeStruct((rows, width), BF16)] * 2
        + [jax.ShapeDtypeStruct((ff, rows), BF16)] * 3,
        compiler_params=params("arbitrary"),
        cost_estimate=cost(12 * rows * width * ff, 10 * rows * width + 6 * width * ff + 6 * rows * ff, rows * ff),
        name="shared_expert",
    )(x_all, dy_all, wz, w_three)


def expert_chunks(ff):
    edges = list(range(0, ff, 256)) + [ff]
    return list(zip(edges[:-1], edges[1:]))


def expert_body(
    meta_ref, place_ref, x_all_ref, dy_all_ref, router_ref, gu_hbm, down_hbm,
    back_ref, routed_ref, d_both_ref, x_t_ref, h_t_ref, d_out_ref,
    gu, down, x_ref, dy_ref, weight_ref, out_acc, in_acc, sems,
):
    ff = EXPERT_FF
    step = pl.program_id(0)
    last = pl.num_programs(0) - 1
    sources, tokens, width = x_all_ref.shape
    slots = x_ref.shape[0] // sources
    shards, _, gu_rows, _ = gu_hbm.shape
    down_rows = down_hbm.shape[2]
    spans = expert_chunks(ff)
    expert = meta_ref[0] * pl.num_programs(0) + step

    def copies(which, at, lo, hi):
        return [
            pltpu.make_async_copy(
                gu_hbm.at[:, which, :, pl.ds(base, hi - lo)],
                gu.at[:, :, pl.ds(base, hi - lo)],
                sems.at[2 * at + part],
            )
            for part, base in enumerate((lo, ff + lo))
        ]

    def down_copies(which):
        return [
            pltpu.make_async_copy(
                down_hbm.at[s, which],
                down.at[pl.ds(s * down_rows, down_rows)],
                sems.at[2 * len(spans) + s],
            )
            for s in range(shards)
        ]

    @pl.when(step == 0)
    def _():
        for at, (lo, hi) in enumerate(spans):
            for copy in copies(0, at, lo, hi):
                copy.start()
            if at == 0:
                for copy in down_copies(0):
                    copy.start()
        back_ref[...] = jnp.zeros_like(back_ref)
        routed_ref[...] = jnp.zeros_like(routed_ref)

    slot_line = lax.broadcasted_iota(jnp.int32, (slots, tokens), 0)

    def chosen(k):
        return slot_line == place_ref[0, k : k + 1, :]

    for k in range(sources):
        rows = slice(k * slots, (k + 1) * slots)
        mask = chosen(k)
        one_hot = jnp.where(mask, 1.0, 0.0).astype(BF16)
        source = x_all_ref[k]
        x_ref[rows] = dot(one_hot, source, NN).astype(BF16)
        dy_ref[rows] = dot(one_hot, dy_all_ref[k], NN).astype(BF16)
        logits = dot(router_ref[...], source, NT)
        expo = jnp.exp(logits - jnp.max(logits, axis=0, keepdims=True))
        router = expo / jnp.sum(expo, axis=0, keepdims=True)
        own = lax.broadcasted_iota(jnp.int32, router.shape, 0) == expert
        own = jnp.sum(jnp.where(own, router, 0.0), axis=0, keepdims=True)
        weight_ref[rows] = jnp.sum(jnp.where(mask, own, 0.0), axis=1, keepdims=True)
    x = x_ref[...]
    weight = weight_ref[...]
    d_out = (weight * dy_ref[...].astype(F32)).astype(BF16)
    d_out_ref[0] = d_out
    x_t_ref[0] = x.T
    for at, (lo, hi) in enumerate(spans):
        for copy in copies(0, at, lo, hi):
            copy.wait()
        if at == 0:
            for copy in down_copies(0):
                copy.wait()
        w_gate = gu[:, :, lo:hi].reshape(width, hi - lo)
        w_up = gu[:, :, ff + lo : ff + hi].reshape(width, hi - lo)
        w_down = down[lo:hi]
        gate = dot(x, w_gate, NN)
        up = dot(x, w_up, NN)
        sig = logistic(gate)
        act = gate * sig
        hidden = (act * up).astype(BF16)
        h_t_ref[0, lo:hi] = hidden.T
        d_h = dot(d_out, w_down, NT)
        d_gate = (d_h * up * (sig * (1.0 + gate * (1.0 - sig)))).astype(BF16)
        d_up = (d_h * act).astype(BF16)
        d_both_ref[0, :, lo:hi] = d_gate
        d_both_ref[0, :, ff + lo : ff + hi] = d_up
        out_new = dot(hidden, w_down, NN)
        in_new = dot(d_gate, w_gate, NT) + dot(d_up, w_up, NT)
        if at == 0:
            out_acc[...] = out_new
            in_acc[...] = in_new
        else:
            out_acc[...] += out_new
            in_acc[...] += in_new

        @pl.when(step < last)
        def _():
            for copy in copies(step + 1, at, lo, hi):
                copy.start()
            if at == len(spans) - 1:
                for copy in down_copies(step + 1):
                    copy.start()

    e_out = out_acc[...].astype(BF16).astype(F32)
    d_weight = jnp.sum(dy_ref[...].astype(F32) * e_out, axis=1, keepdims=True)
    mixed = (weight * e_out).astype(BF16)
    d_in = in_acc[...].astype(BF16)
    lane = lax.broadcasted_iota(jnp.int32, (slots, LANES), 1)
    for k in range(sources):
        rows = slice(k * slots, (k + 1) * slots)
        one_hot = jnp.where(chosen(k), 1.0, 0.0).astype(BF16)
        spread = jnp.where(lane == expert, d_weight[rows], 0.0).astype(BF16)
        for ref, cols, value in (
            (routed_ref, slice(0, width), mixed[rows]),
            (back_ref, slice(0, width), d_in[rows]),
            (back_ref, slice(width, width + LANES), spread),
        ):
            so_far = ref[k, :, cols].astype(F32)
            ref[k, :, cols] = (so_far + dot(one_hot, value, TN)).astype(BF16)


def expert_pass(place, x_all, dy_all, w_router, gate_up, down, expert_at, slots):
    sources, tokens, width = x_all.shape
    local = gate_up.shape[1]
    ff = EXPERT_FF
    rows = sources * slots
    n = len(expert_chunks(ff))
    once = lambda *shape: pl.BlockSpec(
        shape, lambda e, m: (0,) * len(shape), pipeline_mode=pl.Buffered(1)
    )
    each = lambda *shape: pl.BlockSpec((1,) + shape, lambda e, m: (e,) + (0,) * len(shape))
    hbm = pl.BlockSpec(memory_space=pl.ANY)
    return pl.pallas_call(
        expert_body,
        grid_spec=pltpu.PrefetchScalarGridSpec(
            num_scalar_prefetch=1,
            grid=(local,),
            in_specs=[
                each(sources, tokens),
                once(sources, tokens, width),
                once(sources, tokens, width),
                once(*w_router.shape),
                hbm,
                hbm,
            ],
            out_specs=[
                once(sources, tokens, width + LANES),
                once(sources, tokens, width),
                each(rows, 2 * ff),
                each(width, rows),
                each(ff, rows),
                each(rows, width),
            ],
            scratch_shapes=[
                pltpu.VMEM((gate_up.shape[0], gate_up.shape[2], 2 * ff), BF16),
                pltpu.VMEM((ff, width), BF16),
                pltpu.VMEM((rows, width), BF16),
                pltpu.VMEM((rows, width), BF16),
                pltpu.VMEM((rows, 1), F32),
                pltpu.VMEM((rows, width), F32),
                pltpu.VMEM((rows, width), F32),
                pltpu.SemaphoreType.DMA((2 * n + gate_up.shape[0],)),
            ],
        ),
        out_shape=[
            jax.ShapeDtypeStruct((sources, tokens, width + LANES), BF16),
            jax.ShapeDtypeStruct((sources, tokens, width), BF16),
            jax.ShapeDtypeStruct((local, rows, 2 * ff), BF16),
            jax.ShapeDtypeStruct((local, width, rows), BF16),
            jax.ShapeDtypeStruct((local, ff, rows), BF16),
            jax.ShapeDtypeStruct((local, rows, width), BF16),
        ],
        compiler_params=params("arbitrary"),
        cost_estimate=cost(
            12 * local * rows * width * ff,
            local * (6 * width * ff + 8 * rows * width + 6 * rows * ff),
            local * rows * ff,
        ),
        name="expert_pass",
    )(expert_at.reshape(1), place, x_all, dy_all, w_router, gate_up, down)


def rope_tables(positions):
    half = HEAD_DIM // 2
    freq = ROPE_BASE ** (-jnp.arange(half, dtype=F32) * 2.0 / HEAD_DIM)
    angle_tab = positions.astype(F32)[:, None] * freq[None, :]
    cosine = jnp.cos(angle_tab)
    sine = jnp.sin(angle_tab)
    return (jnp.concatenate([cosine, cosine], 1), jnp.concatenate([-sine, sine], 1))


def softmax_rows(scores):
    top = jnp.max(scores, axis=-1, keepdims=True)
    expo = jnp.exp(scores - top)
    return expo / jnp.sum(expo, axis=-1, keepdims=True)


def after(value, *others):
    return lax.optimization_barrier((value,) + others)[0]


def add(left, right):
    return left.astype(F32) + right.astype(F32)


def swap(array, bits, axis="shard"):
    count = lax.axis_size(axis)
    return lax.ppermute(array, axis, [(i, i ^ bits) for i in range(count)])


def gather_shard(array):
    if lax.axis_size("shard") != 8:
        return lax.all_gather(array, "shard", axis=0, tiled=True), array
    half = array.shape[0] // 2
    top, low = array[:half], array[half:]
    top_x = swap(top, 2)
    low_y = swap(low, 4)
    own_c = swap(array, 1)
    top_y2 = swap(jnp.concatenate([top, top_x], 0), 4)
    low_x2 = swap(jnp.concatenate([low, low_y], 0), 2)
    near_c = swap(jnp.concatenate([top_x, low_y], 0), 1)
    far_c = swap(jnp.concatenate([top_y2, low_x2], 0), 1)
    top_y, top_xy = top_y2[:half], top_y2[half:]
    low_x, low_xy = low_x2[:half], low_x2[half:]
    top_xc, low_yc = near_c[:half], near_c[half:]
    top_yc, top_xyc, low_xc, low_xyc = [far_c[i * half : (i + 1) * half] for i in range(4)]
    joined = jnp.concatenate(
        [array, own_c, top_x, low_x, top_xc, low_xc, top_y, low_y, top_yc, low_yc]
        + [top_xy, low_xy, top_xyc, low_xyc],
        0,
    )
    return joined, top_x


def gather_small(array):
    if lax.axis_size("shard") != 8:
        return lax.all_gather(array, "shard", axis=0, tiled=False)
    parts = array[None]
    for bits in (1, 2, 4):
        parts = jnp.concatenate([parts, swap(parts, bits)], 0)
    return reorder(parts)


def block_of():
    order = jnp.arange(lax.axis_size("shard"), dtype=jnp.int32)
    return lax.axis_index("shard") ^ order if lax.axis_size("shard") == 8 else order


def reorder(array):
    if lax.axis_size("shard") != 8:
        return array
    own = lax.axis_index("shard")
    return jnp.concatenate([lax.dynamic_slice_in_dim(array, own ^ r, 1, 0) for r in range(8)], 0)


def scatter_shard(blocks):
    if lax.axis_size("shard") != 8:
        return lax.psum_scatter(blocks, "shard", scatter_dimension=0, tiled=False).astype(F32)
    cut = blocks.reshape((2, 2, 2) + blocks.shape[1:])
    both = add(cut[:, :, 0], swap(cut[:, :, 1], 1)).astype(BF16)
    half = blocks.shape[1] // 2
    top, low = both[:, :, :half], both[:, :, half:]
    top = add(top[:, 0], swap(top[:, 1], 2)).astype(BF16)
    low = add(low[0], swap(low[1], 4)).astype(BF16)
    top = add(top[0], swap(top[1], 4))
    low = add(low[0], swap(low[1], 2))
    return jnp.concatenate([top, low], 0)


def turn(array, step):
    count = lax.axis_size("expert")
    return lax.ppermute(array, "expert", [(i, (i + step) % count) for i in range(count)])


def gather_expert(array):
    return jnp.stack([array] + [turn(array, k) for k in range(1, lax.axis_size("expert"))], 0)


def return_expert(blocks):
    total = blocks[0].astype(F32)
    for k in range(1, lax.axis_size("expert")):
        total = total + turn(blocks[k], -k).astype(F32)
    return total


def sum_small(array, *axes):
    for axis in axes:
        bits = 1
        while bits < lax.axis_size(axis):
            array = array + swap(array, bits, axis)
            bits *= 2
    return array


def sum_expert(pieces):
    if lax.axis_size("expert") != 4:
        return [lax.psum(piece, "expert").astype(F32) for piece in pieces]
    place = lax.axis_index("expert")
    inner = (place == 1) | (place == 2)
    sums, before = [], None
    for piece in pieces:
        outer = lax.ppermute(piece, "expert", [(0, 1), (3, 2)])
        if before is not None:
            outer = after(outer, before)
        side = add(piece, outer).astype(BF16)
        other = lax.ppermute(side, "expert", [(1, 2), (2, 1)])
        total = add(side, other).astype(BF16)
        before = total
        back = lax.ppermute(total, "expert", [(1, 0), (2, 3)])
        sums.append(jnp.where(inner, total, back).astype(F32))
    return sums


def per_device(
    tokens,
    attn_gain,
    qkv_weight,
    qkv_bias,
    out_weight,
    ffn_gain,
    router_weight,
    shared_gate_weight,
    shared_weights,
    expert_gate_up,
    expert_down,
    routes,
    arrival,
    cotangent,
):
    shard_count = lax.axis_size("shard")
    expert_count = lax.axis_size("expert")
    shard_at = lax.axis_index("shard")
    expert_at = lax.axis_index("expert")
    rows_local = tokens.shape[0]
    width = tokens.shape[1]
    group_rows = rows_local * shard_count
    prompt_len = group_rows // 2
    local_experts = expert_gate_up.shape[1]
    experts_all = local_experts * expert_count
    capacity = rows_local * TOPK // experts_all
    blocks = block_of()

    tokens_all, started = gather_shard(tokens)
    params_own = jnp.concatenate(
        [attn_gain[None], ffn_gain[None], shared_gate_weight[None], router_weight.T], 0
    )
    params_all = jnp.moveaxis(gather_small(params_own), 0, 1).reshape(-1, width)
    gain_one_f = params_all[0:1].astype(F32)
    gain_two_f = params_all[1:2].astype(F32)
    w_zgate = params_all[2:3]
    w_router = params_all[3:]

    gate_up_own = jnp.moveaxis(after(expert_gate_up, started), 1, 0)
    down_own = jnp.moveaxis(after(expert_down, started), 1, 0)
    w_gate_up = lax.all_gather(gate_up_own, "shard", axis=0, tiled=False)
    w_down = lax.all_gather(down_own, "shard", axis=0, tiled=False)

    route_flat = routes.reshape(-1)
    priority = arrival.reshape(-1)
    same_expert = route_flat[:, None] == route_flat[None, :]
    earlier = priority[None, :] < priority[:, None]
    ranks = jnp.sum((same_expert & earlier).astype(jnp.int32), axis=1)
    kept_rank = jnp.where(ranks < capacity, ranks + 1, 0).reshape(rows_local, TOPK)
    expert_ids = jnp.arange(experts_all, dtype=jnp.int32)
    place = (
        jnp.sum(
            jnp.where(routes[:, :, None] == expert_ids[None, None, :], kept_rank[:, :, None], 0), 1
        )
        - 1
    )
    place_z = gather_expert(place.T)
    place_own = jnp.moveaxis(
        lax.dynamic_slice_in_dim(place_z, expert_at * local_experts, local_experts, 1), 1, 0
    )
    dy_z = gather_expert(cotangent)
    dy_all, _ = gather_shard(after(cotangent, tokens_all))

    line = jnp.arange(group_rows, dtype=jnp.int32)
    position = jnp.where(line < prompt_len, line, prompt_len + (line - prompt_len) % rows_local)
    cosine, sine = rope_tables(position)
    w_three = jnp.swapaxes(qkv_weight, 0, 1)
    qkv, attn_t = qkv_forward(
        tokens_all, gain_one_f, w_three, qkv_bias, cosine, sine, blocks, rows_local
    )
    context, context_t = attend_forward(qkv, blocks, rows_local, prompt_len)
    attn_part = dot(context, out_weight, NN).astype(BF16)
    x_float = tokens.astype(F32)
    hidden_state = x_float + scatter_shard(attn_part.reshape(shard_count, rows_local, width))

    inv_two = lax.rsqrt(jnp.mean(hidden_state * hidden_state, axis=1, keepdims=True) + EPSILON)
    normed_two = hidden_state * inv_two
    ffn_in = (normed_two * gain_two_f).astype(BF16)
    ffn_all, _ = gather_shard(ffn_in)
    ffn_z = gather_expert(ffn_in)
    router = softmax_rows(dot(ffn_in, w_router, NT))
    w_zgate_f = w_zgate.astype(F32)
    z_gate = logistic(jnp.sum(ffn_in.astype(F32) * w_zgate_f, axis=1, keepdims=True))
    d_out = cotangent.astype(F32)

    w_shared = jnp.swapaxes(shared_weights, 1, 2)
    shared_back, out_part, d_so, hidden_t, d_gate_t, d_up_t = shared_expert(
        ffn_all, dy_all, w_zgate_f, w_shared
    )
    shared_back = scatter_shard(shared_back.reshape(shard_count, rows_local, width + LANES))
    grad_shared = [
        dot(d_gate_t, ffn_all, NN).astype(BF16),
        dot(d_up_t, ffn_all, NN).astype(BF16),
        dot(hidden_t, d_so, NN).astype(BF16),
    ]
    shared_out = lax.psum_scatter(
        reorder(out_part.reshape(shard_count, rows_local, width)),
        "shard",
        scatter_dimension=0,
        tiled=False,
    )

    routed_back, routed, d_both, x_t, h_t, d_eout = expert_pass(
        place_own, ffn_z, dy_z, w_router, w_gate_up, w_down, expert_at, capacity
    )
    routed_back = return_expert(routed_back)
    routed = return_expert(routed)
    output = (hidden_state + routed + z_gate * shared_out.astype(F32)).astype(BF16)
    grad_gate_up = [dot(x_t[e], d_both[e], NN).astype(BF16) for e in range(local_experts)]
    grad_down = [dot(h_t[e], d_eout[e], NN).astype(BF16) for e in range(local_experts)]

    d_router = routed_back[:, width : width + experts_all]
    d_logit = (router * (d_router - jnp.sum(d_router * router, axis=1, keepdims=True))).astype(BF16)
    grad_router = dot(d_logit, ffn_in, TN)
    d_zlogit = shared_back[:, width : width + 1] * z_gate * (1.0 - z_gate)
    grad_zgate = jnp.sum(d_zlogit * ffn_in.astype(F32), axis=0)
    d_ffn = (
        shared_back[:, :width]
        + routed_back[:, :width]
        + dot(d_logit, w_router, NN)
        + d_zlogit * w_zgate_f
    )
    grad_gain_two = jnp.sum(d_ffn * normed_two, axis=0)
    d_norm_two = d_ffn * gain_two_f
    d_hidden = d_out + inv_two * (
        d_norm_two - normed_two * jnp.mean(d_norm_two * normed_two, axis=1, keepdims=True)
    )
    d_ao_all, _ = gather_shard(d_hidden.astype(BF16))

    d_ctx = dot(d_ao_all, out_weight, NT).astype(BF16)
    d_qkv = attend_backward(qkv, d_ctx, cosine, sine, blocks, rows_local, prompt_len)
    d_in_part = input_grad(d_qkv, w_three)
    d_attn_in = scatter_shard(d_in_part.reshape(shard_count, rows_local, width))
    grad_out = dot(context_t, d_ao_all, NN).astype(BF16)
    grad_qkv = [dot(attn_t, d_qkv[part], NN).astype(BF16) for part in range(3)]
    grad_bias = jnp.sum(d_qkv.astype(F32), axis=1)
    inv_one = lax.rsqrt(jnp.mean(x_float * x_float, axis=1, keepdims=True) + EPSILON)
    normed_one = x_float * inv_one
    grad_gain_one = jnp.sum(d_attn_in * normed_one, axis=0)
    d_norm_one = d_attn_in * gain_one_f
    tokens_grad = (
        d_hidden
        + inv_one
        * (d_norm_one - normed_one * jnp.mean(d_norm_one * normed_one, axis=1, keepdims=True))
    ).astype(BF16)

    g_egu = jnp.stack(
        [lax.psum_scatter(g, "shard", scatter_dimension=0, tiled=True) for g in grad_gate_up], 1
    ).astype(F32)
    g_edown = jnp.stack(
        [lax.psum_scatter(g, "shard", scatter_dimension=0, tiled=True) for g in grad_down], 1
    ).astype(F32)
    s_down, s_gate, s_up, g_out, g_q, g_k, g_v = sum_expert(
        [grad_shared[2], grad_shared[0], grad_shared[1], grad_out] + grad_qkv
    )
    g_shared = jnp.swapaxes(jnp.stack([s_gate, s_up, s_down]), 1, 2)
    g_qkv = jnp.swapaxes(jnp.stack([g_q, g_k, g_v]), 0, 1)
    own_cols = lambda a: lax.dynamic_slice_in_dim(
        a, shard_at * (width // shard_count), width // shard_count, 1
    )
    small = own_cols(
        sum_small(
            jnp.concatenate([grad_router, grad_zgate[None], grad_gain_two[None]], 0),
            "shard",
            "expert",
        )
    )
    g_router = small[:experts_all].T
    g_zgate = small[experts_all]
    g_gain_two = small[experts_all + 1]
    g_gain_one = own_cols(sum_small(grad_gain_one[None], "shard", "expert"))[0]
    g_bias = sum_small(grad_bias, "expert")
    return (
        output,
        tokens_grad,
        g_gain_one,
        g_qkv,
        g_bias,
        g_out,
        g_gain_two,
        g_router,
        g_zgate,
        g_shared,
        g_egu,
        g_edown,
    )


def solution(mesh):
    placed = (
        P(("expert", "shard"), None),
        P("shard"),
        P(None, None, "shard"),
        P(None, "shard"),
        P("shard", None),
        P("shard"),
        P("shard", None),
        P("shard"),
        P(None, None, "shard"),
        P("shard", "expert", None),
        P("shard", "expert", None),
        P(("expert", "shard"), None),
        P(("expert", "shard"), None),
        P(("expert", "shard"), None),
    )
    return jax.shard_map(
        per_device,
        mesh=mesh,
        in_specs=placed,
        out_specs=(
            P(("expert", "shard"), None),
            P(("expert", "shard"), None),
            P("shard"),
            P(None, None, "shard"),
            P(None, "shard"),
            P("shard", None),
            P("shard"),
            P("shard", None),
            P("shard"),
            P(None, None, "shard"),
            P("shard", "expert", None),
            P("shard", "expert", None),
        ),
        check_vma=False,
    )
```
